512 devices in a mesh: replica: 32 (over z_lo, y, core), fsdp: 16 (over x, z_hi).
Axes of the slice: x: 4, y: 8, z: 8 (z_hi: 4, z_lo: 2; z = z_hi * 2 + z_lo), core: 2. Of those that a mesh axis runs over, the one named last changes fastest.
Arguments:
- activations: bfloat16 [32, 7168, 4096], P('replica', 'fsdp'), may hold values from -84 to 84
- targets: bfloat16 [32, 7168, 512], P('replica', 'fsdp'), may hold values from -8 to 8
- weights: float32 [32, 4096, 512], P('replica', 'fsdp'), may hold values from -19 to 19
- lengths: int32 [32, 112], P('replica'), may hold values from 1 to 64, 3584 in all within a row
Outputs:
- averaged: float32 [32, 4096, 512], P('replica', 'fsdp')
The draws below stay inside these ranges and needn't reach their ends.
Inputs may be any that keep to these rules, and one draw needn't show every extreme that they name: `lengths`: each row sums to 3584; sequence s of a replica fills slot s from its first position.
All inputs are finite; a program needn't handle non-finite values.
Results may differ from the reference program's by a relative error of at most 0.0014.
Values may be sent and summed in bfloat16 or wider, within the bound.
A program may use at most 64 MiB of HBM per device.

```python
import math
import jax
import jax.numpy as jnp
import numpy as np
from jax import lax

D = 4096
KV = 512
SLOT = 64
STEP = 3
TOK_DEV = 448
TOKENS = 7168
NSEQ = 112
LIVE = 3584
N_REPLICA = 32
N_FSDP = 16


def draw_activations(key, part):
    base_key, rough_key = jax.random.split(jax.random.fold_in(key, 7), 2)
    ramp = 10.0 ** (jnp.arange(D, dtype=jnp.float32) / D)
    rough = jax.random.uniform(rough_key, (D,), jnp.float32, 0.7, 1.4)
    base = jax.random.normal(base_key, (N_REPLICA, TOKENS, D), jnp.float32)
    base = jnp.clip(base, -6.0, 6.0)
    return (base * (ramp * rough)).astype(jnp.bfloat16)


def draw_weights(key, part):
    base_key, column_key = jax.random.split(jax.random.fold_in(key, 13), 2)
    column_scale = 10.0 ** jax.random.uniform(column_key, (N_REPLICA, 1, KV), jnp.float32, -0.5, 0.5)
    base = jnp.clip(jax.random.normal(base_key, (N_REPLICA, D, KV), jnp.float32), -6.0, 6.0)
    return base * column_scale


def levels(stream_key, extent, shards, low, largest):
    def one(dim, blocks):
        draws = jax.random.uniform(jax.random.fold_in(jax.random.fold_in(stream_key, 6), dim), (blocks,), jnp.float32, low / len(shards), largest / len(shards))
        return jnp.repeat(jnp.exp(draws), extent[dim] // blocks).reshape((-1,) + (1,) * (len(extent) - dim - 1))

    gain = one(*shards[0])
    for cut in shards[1:]:
        gain = gain * one(*cut)
    return gain


def length_profile(count, total, limit, lean):
    loads = [(1 << 20) // math.isqrt(rank ** lean) + 1 for rank in range(2, count + 1)]
    rest, given = total - limit - (count - 1), [1] * (count - 1)
    while rest > 0:
        movable = [i for i in range(count - 1) if given[i] < limit]
        whole, remaining = sum([loads[i] for i in movable]), rest
        for i in movable:
            addition = min(limit - given[i], max(1, remaining * loads[i] // whole), rest)
            given[i] = given[i] + addition
            rest = rest - addition
    return np.array([limit] + given)


def uneven_parts(own_key, amount, total, most, lean):
    if amount == 2:
        one = jax.random.randint(own_key, (), max(1, total - most), min(most, total - 1) + 1)
        return jnp.stack([one, total - one])
    tallies = jnp.asarray(length_profile(amount, total, most, lean), jnp.int32)
    pairs = (amount - 1) // 2
    source_of, taker = tallies[1:1 + 2 * pairs:2], tallies[2:2 + 2 * pairs:2]
    margin = jnp.minimum(source_of - 1, most - taker)
    shifted = jax.random.randint(jax.random.fold_in(own_key, 1), (pairs,), 0, 1 << 20) % (margin + 1)
    tallies = tallies.at[1:1 + 2 * pairs:2].set(source_of - shifted).at[2:2 + 2 * pairs:2].set(taker + shifted)
    return tallies[jax.random.permutation(jax.random.fold_in(own_key, 2), amount)]


def gaussian(own_key, extent, spread, bound, shards=(), kind=jnp.bfloat16):
    loudness = levels(own_key, extent, shards, -0.22, 0.18) if shards else 1.0
    array = jax.random.normal(own_key, extent, jnp.float32) * spread * loudness
    return jnp.minimum(jnp.maximum(array, -bound), bound).astype(kind)


def setup_inputs(seed: int = 0) -> dict:
    streams_of = jax.random.split(jax.random.key(seed), 5)
    return {
        "activations": draw_activations(jax.random.fold_in(streams_of[4], 71), 0),
        "targets": gaussian(streams_of[1], (N_REPLICA, TOKENS, KV), 2.0, 8.0, ((0, 32), (1, 16))),
        "weights": draw_weights(jax.random.fold_in(streams_of[4], 71), 0),
        "lengths": jax.vmap(lambda own: uneven_parts(own, NSEQ, LIVE, SLOT, 2))(jax.random.split(streams_of[3], N_REPLICA)).reshape((N_REPLICA, NSEQ)).astype(jnp.int32),
    }


learning_rate = 0.1
epsilon = 1e-06

def replica_update(features, wanted, master, lengths_row):
    keys_out = jnp.dot(features, master.astype(jnp.bfloat16), preferred_element_type=jnp.float32) * D ** (-0.5)
    positions = jnp.arange(TOKENS, dtype=jnp.int32)
    sequence_ids = (positions // SLOT).astype(jnp.int32)
    own_lengths = jnp.take(lengths_row, sequence_ids)
    live_mask = positions % SLOT < own_lengths
    residual = jnp.where(live_mask[:, None], keys_out - wanted.astype(jnp.float32), 0.0).astype(jnp.bfloat16)
    grouped_features = features.reshape(N_FSDP, TOK_DEV, D).astype(jnp.float32)
    grouped_residual = residual.reshape(N_FSDP, TOK_DEV, KV).astype(jnp.float32)
    partials = jnp.einsum('ftd,ftk->fdk', grouped_features, grouped_residual)
    rounded = lax.optimization_barrier(partials.astype(jnp.bfloat16))
    gradient = lax.optimization_barrier(jnp.sum(rounded.astype(jnp.float32), axis=0))
    square_sum = jnp.sum(gradient * gradient)
    direction = gradient * lax.rsqrt(square_sum / (D * KV) + epsilon)
    return master - learning_rate * direction

def reference(activations, targets, weights, lengths):
    updated = lax.map(lambda items: replica_update(items[0], items[1], items[2], items[3]), (activations, targets, weights, lengths))
    distance_bit = STEP % (N_REPLICA.bit_length() - 1)
    partner_ids = jnp.bitwise_xor(jnp.arange(N_REPLICA, dtype=jnp.int32), 1 << distance_bit).astype(jnp.int32)
    return 0.5 * (updated + updated[partner_ids])
```

```python
import functools

import jax
import jax.numpy as jnp
from jax import lax
from jax.experimental import pallas as pl
from jax.experimental.pallas import tpu as pltpu
from jax.sharding import PartitionSpec as P

SLOT = 64
STEP = 3
LANES = 128
SIDE = 4

learning_rate = 0.1
epsilon = 1e-06

MESH = pl.DeviceIdType.MESH
FIRST = ("z", "z", "x", "z")


def kernel(
    bit,
    act,
    tgt,
    wgt,
    lens,
    out,
    a_v,
    at_v,
    t_v,
    wm,
    wp,
    w_all,
    keys,
    res,
    relay_out,
    relay_in,
    relay_own,
    fin_out_p,
    fin_out_m,
    fin_in_p,
    fin_in_m,
    own1,
    s2_out,
    s2_rin,
    f2_out_p,
    f2_out_m,
    f2_in_p,
    f2_in_m,
    g,
    gp,
    ss,
    ss_x,
    ss_xs,
    ss_z,
    ss_zs,
    ss_y,
    load_sem,
    ag_s,
    ag_r,
    rs_s,
    rs_r,
    y_s,
    y_r,
    ps_s,
    ps_r,
):
    members, tokens, rows = a_v.shape[0], act.shape[0], a_v.shape[2]
    depth = act.shape[1]
    chunks = w_all.shape[0]
    half = rows // 2
    sequences = tokens // SLOT
    fs = lax.axis_index("fsdp")
    rep = lax.axis_index("replica")
    x = lax.div(fs, SIDE)
    z = lax.rem(fs, SIDE)
    mask = 2**bit
    partner = rep + mask - 2 * mask * lax.rem(lax.div(rep, mask), 2)

    def step(v, k):
        return lax.rem(v + k, SIDE)

    def member(c, df, ds):
        if FIRST[c] == "z":
            return step(x, ds) * SIDE + step(z, df)
        return step(x, df) * SIDE + step(z, ds)

    load_w = pltpu.make_async_copy(wgt, wm, load_sem.at[members])
    load_w.start()
    load_t = pltpu.make_async_copy(tgt, t_v, load_sem.at[members + 1])
    load_t.start()
    load_a = []
    for m in range(members):
        load_a.append(
            pltpu.make_async_copy(
                act.at[:, pl.ds(m * rows, rows)],
                a_v.at[m, pl.ds(0, tokens), :],
                load_sem.at[m],
            )
        )
        load_a[-1].start()

    barrier = pltpu.get_barrier_semaphore()
    peers_x = [{"fsdp": step(x, k) * SIDE + z} for k in range(1, SIDE)]
    peers_z = [{"fsdp": x * SIDE + step(z, k)} for k in range(1, SIDE)]
    peer_y = {"replica": partner}
    for peer in peers_x + peers_z + [peer_y]:
        pl.semaphore_signal(barrier, inc=1, device_id=peer, device_id_type=MESH)

    load_w.wait()
    for c in range(chunks):
        w_all[c, fs] = wm[:, c * LANES : (c + 1) * LANES].astype(jnp.bfloat16)
    if a_v.shape[1] > tokens:
        pad = a_v.shape[1] - tokens
        res[pl.ds(tokens, pad), :] = jnp.zeros((pad, LANES), res.dtype)
        for m in range(members):
            a_v[m, pl.ds(tokens, pad), :] = jnp.zeros((pad, rows), a_v.dtype)
    pl.semaphore_wait(barrier, len(peers_x) + len(peers_z) + 1)

    sent = []

    def send(src, dst, send_sem, recv_sem, to):
        copy = pltpu.make_async_remote_copy(
            src_ref=src,
            dst_ref=dst,
            send_sem=send_sem,
            recv_sem=recv_sem,
            device_id=to,
            device_id_type=MESH,
        )
        copy.start()
        sent.append(copy)

    def arrived(dst, send_sem, recv_sem, to):
        pltpu.make_async_remote_copy(
            src_ref=dst,
            dst_ref=dst,
            send_sem=send_sem,
            recv_sem=recv_sem,
            device_id=to,
            device_id_type=MESH,
        ).wait_recv()

    def to_f(c, k):
        return {"fsdp": member(c, k, 0)}

    def to_s(c, k):
        return {"fsdp": member(c, 0, k)}

    def spread(c, j):
        block = w_all.at[c, member(c, j, 0)]
        send(block, block, ag_s.at[c, 4 + j], ag_r.at[c, 4 + j], to_s(c, 1))
        send(block, block, ag_s.at[c, 8 + j], ag_r.at[c, 8 + j], to_s(c, 3))

    def gather_start(c):
        block = w_all.at[c, fs]
        send(block, block, ag_s.at[c, 0], ag_r.at[c, 0], to_f(c, 1))
        send(block, block, ag_s.at[c, 1], ag_r.at[c, 1], to_f(c, 3))
        spread(c, 0)

    def gather_first(c):
        block = w_all.at[c, member(c, 3, 0)]
        arrived(block, ag_s.at[c, 0], ag_r.at[c, 0], to_f(c, 1))
        part = block.at[pl.ds(0, half), :]
        send(part, part, ag_s.at[c, 2], ag_r.at[c, 2], to_f(c, 1))
        spread(c, 3)
        block = w_all.at[c, member(c, 1, 0)]
        arrived(block, ag_s.at[c, 1], ag_r.at[c, 1], to_f(c, 3))
        part = block.at[pl.ds(half, half), :]
        send(part, part, ag_s.at[c, 3], ag_r.at[c, 3], to_f(c, 3))
        spread(c, 1)

    def project(c, ds, fresh=False):
        def body(j, carry):
            m = member(c, j, ds)
            keys[c] += jnp.dot(
                a_v[m, pl.ds(0, tokens), :], w_all[c, m], preferred_element_type=jnp.float32
            )
            return carry

        if fresh:
            keys[c] = jnp.zeros((tokens, LANES), jnp.float32)
        lax.fori_loop(0, SIDE, body, 0)

    def gather_far(c):
        block = w_all.at[c, member(c, 2, 0)]
        arrived(block.at[pl.ds(0, half), :], ag_s.at[c, 2], ag_r.at[c, 2], to_f(c, 1))
        arrived(block.at[pl.ds(half, half), :], ag_s.at[c, 3], ag_r.at[c, 3], to_f(c, 3))
        spread(c, 2)
        project(c, 0, fresh=True)

    def gather_second(c):
        for j in (0, 3, 1, 2):
            block = w_all.at[c, member(c, j, 3)]
            arrived(block, ag_s.at[c, 4 + j], ag_r.at[c, 4 + j], to_s(c, 1))
            if j < 2:
                send(block, block, ag_s.at[c, 12 + j], ag_r.at[c, 12 + j], to_s(c, 1))
            block = w_all.at[c, member(c, j, 1)]
            arrived(block, ag_s.at[c, 8 + j], ag_r.at[c, 8 + j], to_s(c, 3))
            if j >= 2:
                send(block, block, ag_s.at[c, 12 + j], ag_r.at[c, 12 + j], to_s(c, 3))
        project(c, 3)
        project(c, 1)

    def times_residual(c, j, ds):
        return jnp.dot(at_v[member(c, j, ds)], res[...], preferred_element_type=jnp.float32)

    def differentiate(c):
        for j in range(SIDE):
            block = w_all.at[c, member(c, j, 2)]
            arrived(block, ag_s.at[c, 12 + j], ag_r.at[c, 12 + j], to_s(c, 1 if j < 2 else 3))
        project(c, 2)
        for k in range(sequences):
            span = pl.ds(k * SLOT, SLOT)
            live = lax.broadcasted_iota(jnp.int32, (SLOT, LANES), 0) < lens[fs * sequences + k]
            wanted = t_v[span, c * LANES : (c + 1) * LANES].astype(jnp.float32)
            keys_out = keys[c, span, :] * depth ** (-0.5)
            res[span, :] = jnp.where(live, keys_out - wanted, 0.0).astype(jnp.bfloat16)

        def far(j, carry):
            relay_out[c, j] = times_residual(c, j, 2).astype(jnp.bfloat16)
            return carry

        def plus(j, carry):
            fin_out_p[c, j] = times_residual(c, j, 1).astype(jnp.bfloat16)
            return carry

        def minus(j, carry):
            fin_out_m[c, j] = times_residual(c, j, 3).astype(jnp.bfloat16)
            return carry

        def plus_relayed(j, carry):
            relay_own[c, j] = times_residual(c, j, 1)
            return carry

        def minus_relayed(j, carry):
            relay_own[c, j] = times_residual(c, j, 3)
            return carry

        def here(j, carry):
            own1[c, j] = times_residual(c, j, 0)
            return carry

        lax.fori_loop(0, SIDE, far, 0)
        for j in range(SIDE):
            send(
                relay_out.at[c, j],
                relay_in.at[c, j],
                rs_s.at[c, j],
                rs_r.at[c, j],
                to_s(c, 1 if j < 2 else 3),
            )
        lax.fori_loop(2, SIDE, plus, 0)
        for j in (2, 3):
            send_plus(c, j)
        lax.fori_loop(0, 2, minus, 0)
        for j in (0, 1):
            send_minus(c, j)
        lax.fori_loop(0, 2, plus_relayed, 0)
        lax.fori_loop(2, SIDE, minus_relayed, 0)
        lax.fori_loop(0, SIDE, here, 0)

    def send_plus(c, j):
        send(
            fin_out_p.at[c, j], fin_in_m.at[c, j], rs_s.at[c, 4 + j], rs_r.at[c, 4 + j], to_s(c, 1)
        )

    def send_minus(c, j):
        send(
            fin_out_m.at[c, j], fin_in_p.at[c, j], rs_s.at[c, 8 + j], rs_r.at[c, 8 + j], to_s(c, 3)
        )

    def reduce_relay(c):
        for j in (2, 1, 3, 0):
            arrived(
                relay_in.at[c, j], rs_s.at[c, j], rs_r.at[c, j], to_s(c, 1 if j < 2 else 3)
            )
            total = (relay_own[c, j] + relay_in[c, j].astype(jnp.float32)).astype(jnp.bfloat16)
            if j < 2:
                fin_out_p[c, j] = total
                send_plus(c, j)
            else:
                fin_out_m[c, j] = total
                send_minus(c, j)

    def reduce_second(c):
        for j in (2, 1, 3, 0):
            arrived(fin_in_m.at[c, j], rs_s.at[c, 4 + j], rs_r.at[c, 4 + j], to_s(c, 1))
            arrived(fin_in_p.at[c, j], rs_s.at[c, 8 + j], rs_r.at[c, 8 + j], to_s(c, 3))
            total = (
                own1[c, j]
                + fin_in_m[c, j].astype(jnp.float32)
                + fin_in_p[c, j].astype(jnp.float32)
            )
            if j == 2:
                s2_out[c] = total.astype(jnp.bfloat16)
                send(
                    s2_out.at[c, pl.ds(0, half), :],
                    s2_rin.at[c, 0],
                    rs_s.at[c, 12],
                    rs_r.at[c, 12],
                    to_f(c, 1),
                )
                send(
                    s2_out.at[c, pl.ds(half, half), :],
                    s2_rin.at[c, 1],
                    rs_s.at[c, 13],
                    rs_r.at[c, 13],
                    to_f(c, 3),
                )
            else:
                own1[c, j] = total

    def reduce_far(c):
        upper, lower = pl.ds(0, half), pl.ds(half, half)
        arrived(s2_rin.at[c, 0], rs_s.at[c, 12], rs_r.at[c, 12], to_f(c, 1))
        f2_out_p[c, upper, :] = (
            own1[c, 1, upper, :] + s2_rin[c, 0].astype(jnp.float32)
        ).astype(jnp.bfloat16)
        f2_out_p[c, lower, :] = own1[c, 1, lower, :].astype(jnp.bfloat16)
        send(f2_out_p.at[c], f2_in_m.at[c], rs_s.at[c, 14], rs_r.at[c, 14], to_f(c, 1))
        arrived(s2_rin.at[c, 1], rs_s.at[c, 13], rs_r.at[c, 13], to_f(c, 3))
        f2_out_m[c, lower, :] = (
            own1[c, 3, lower, :] + s2_rin[c, 1].astype(jnp.float32)
        ).astype(jnp.bfloat16)
        f2_out_m[c, upper, :] = own1[c, 3, upper, :].astype(jnp.bfloat16)
        send(f2_out_m.at[c], f2_in_p.at[c], rs_s.at[c, 15], rs_r.at[c, 15], to_f(c, 3))

    def reduce_done(c):
        arrived(f2_in_m.at[c], rs_s.at[c, 14], rs_r.at[c, 14], to_f(c, 1))
        arrived(f2_in_p.at[c], rs_s.at[c, 15], rs_r.at[c, 15], to_f(c, 3))
        total = own1[c, 0] + f2_in_m[c].astype(jnp.float32) + f2_in_p[c].astype(jnp.float32)
        g[c] = total
        send(g.at[c], gp.at[c], y_s.at[c], y_r.at[c], peer_y)
        squares = jnp.sum((total * total).reshape(rows // 8, 8, LANES), axis=0)
        done.append(c)
        if len(done) == 1:
            ss[...] = squares
        else:
            ss[...] += squares

    done = []
    gather_start(0)
    gather_start(1)
    send(wm, wp, y_s.at[chunks], y_r.at[chunks], peer_y)
    load_t.wait()
    for m in range(members):
        load_a[m].wait()

    def transpose(m, carry):
        at_v[m] = a_v[m].T
        return carry

    lax.fori_loop(0, members, transpose, 0)

    def gather_first_then_start(c):
        gather_first(c)
        if c + 2 < chunks:
            gather_start(c + 2)

    stages = (
        gather_first_then_start,
        gather_far,
        gather_second,
        differentiate,
        reduce_relay,
        reduce_second,
        reduce_far,
        reduce_done,
    )
    for t in range(chunks + len(stages) - 1):
        for c in range(chunks):
            if 0 <= t - c < len(stages):
                stages[t - c](c)

    for k in range(SIDE - 1):
        send(ss, ss_x.at[k], ps_s.at[k], ps_r.at[k], peers_x[k])
    for k in range(SIDE - 1):
        arrived(ss_x.at[k], ps_s.at[k], ps_r.at[k], peers_x[k])
    ss_xs[...] = ss[...] + ss_x[0] + ss_x[1] + ss_x[2]
    for k in range(SIDE - 1):
        send(ss_xs, ss_z.at[k], ps_s.at[3 + k], ps_r.at[3 + k], peers_z[k])
    for k in range(SIDE - 1):
        arrived(ss_z.at[k], ps_s.at[3 + k], ps_r.at[3 + k], peers_z[k])
    ss_zs[...] = ss_xs[...] + ss_z[0] + ss_z[1] + ss_z[2]
    send(ss_zs, ss_y, ps_s.at[6], ps_r.at[6], peer_y)

    entries = depth * LANES * chunks

    def scale(tile):
        total = jnp.sum(tile, axis=(0, 1), keepdims=True)
        return (0.5 * learning_rate) * lax.rsqrt(total / entries + epsilon)

    own_scale = scale(ss_zs[...])
    arrived(wp, y_s.at[chunks], y_r.at[chunks], peer_y)
    for c in range(chunks):
        cut = slice(c * LANES, (c + 1) * LANES)
        out[:, cut] = 0.5 * (wm[:, cut] + wp[:, cut]) - own_scale * g[c]
    for c in range(chunks):
        arrived(gp.at[c], y_s.at[c], y_r.at[c], peer_y)
    arrived(ss_y, ps_s.at[6], ps_r.at[6], peer_y)
    partner_scale = scale(ss_y[...])
    for c in range(chunks):
        cut = slice(c * LANES, (c + 1) * LANES)
        out[:, cut] = out[:, cut] - partner_scale * gp[c]
    for copy in sent:
        copy.wait_send()


def local(activations, targets, weights, lengths):
    tokens, depth = activations.shape[1:]
    rows, columns = weights.shape[1:]
    members = lax.axis_size("fsdp")
    chunks = columns // LANES
    bit = STEP % (lax.axis_size("replica").bit_length() - 1)
    padded = -(-tokens // LANES) * LANES
    bf16, f32 = jnp.bfloat16, jnp.float32
    vmem = pltpu.VMEM
    dma = pltpu.SemaphoreType.DMA
    block = (rows, LANES)
    any_spec = pl.BlockSpec(memory_space=pl.ANY)
    averaged = pl.pallas_call(
        functools.partial(kernel, bit),
        out_shape=jax.ShapeDtypeStruct((rows, columns), f32),
        in_specs=[any_spec, any_spec, any_spec, pl.BlockSpec(memory_space=pltpu.SMEM)],
        out_specs=pl.BlockSpec(memory_space=pltpu.VMEM),
        scratch_shapes=[
            vmem((members, padded, rows), bf16),
            vmem((members, rows, padded), bf16),
            vmem((tokens, columns), bf16),
            vmem((rows, columns), f32),
            vmem((rows, columns), f32),
            vmem((chunks, members) + block, bf16),
            vmem((chunks, tokens, LANES), f32),
            vmem((padded, LANES), bf16),
            vmem((chunks, SIDE) + block, bf16),
            vmem((chunks, SIDE) + block, bf16),
            vmem((chunks, SIDE) + block, f32),
            vmem((chunks, SIDE) + block, bf16),
            vmem((chunks, SIDE) + block, bf16),
            vmem((chunks, SIDE) + block, bf16),
            vmem((chunks, SIDE) + block, bf16),
            vmem((chunks, SIDE) + block, f32),
            vmem((chunks,) + block, bf16),
            vmem((chunks, 2, rows // 2, LANES), bf16),
            vmem((chunks,) + block, bf16),
            vmem((chunks,) + block, bf16),
            vmem((chunks,) + block, bf16),
            vmem((chunks,) + block, bf16),
            vmem((chunks,) + block, f32),
            vmem((chunks,) + block, f32),
            vmem((8, LANES), f32),
            vmem((3, 8, LANES), f32),
            vmem((8, LANES), f32),
            vmem((3, 8, LANES), f32),
            vmem((8, LANES), f32),
            vmem((8, LANES), f32),
            dma((members + 2,)),
            dma((chunks, 16)),
            dma((chunks, 16)),
            dma((chunks, 16)),
            dma((chunks, 16)),
            dma((chunks + 1,)),
            dma((chunks + 1,)),
            dma((7,)),
            dma((7,)),
        ],
        compiler_params=pltpu.CompilerParams(
            collective_id=0, has_side_effects=True, vmem_limit_bytes=60 * 2**20
        ),
    )(activations[0], targets[0], weights[0], lengths[0])
    return averaged[None]


def solution(mesh):
    return jax.shard_map(
        local,
        mesh=mesh,
        in_specs=(
            P("replica", "fsdp", None),
            P("replica", "fsdp", None),
            P("replica", "fsdp", None),
            P("replica", None),
        ),
        out_specs=P("replica", "fsdp", None),
        check_vma=False,
    )
```

```python
import functools

import jax
import jax.numpy as jnp
from jax import lax
from jax.experimental import pallas as pl
from jax.experimental.pallas import tpu as pltpu
from jax.sharding import PartitionSpec as P

SLOT = 64
STEP = 3
LANES = 128
SIDE = 4

learning_rate = 0.1
epsilon = 1e-06

MESH = pl.DeviceIdType.MESH
FIRST = ("z", "z", "x", "z")
(
    FROM_MINUS,
    FROM_PLUS,
    FIRST_MINUS,
    FIRST_PLUS,
    FIRST_FAR,
    PROJECT_HERE,
    PROJECT_MINUS,
    PROJECT_PLUS,
    PROJECT_FAR,
    GRAD_FAR,
    GRAD_SENT,
    GRAD_RELAYED,
    GRAD_HERE,
    RELAY,
    SECOND,
    FAR_MINUS,
    FAR_PLUS,
    FINISH,
    START,
    TRANSPOSE,
) = range(20)
ORDER = (
    (START, 0, 0), (START, 1, 0), (START, 3, 0), (TRANSPOSE, -1, 2),
    (FIRST_PLUS, 0, 0), (FIRST_MINUS, 0, 0), (START, 2, 0), (FIRST_MINUS, 1, 0),
    (TRANSPOSE, -1, 0), (FIRST_PLUS, 1, 0), (FIRST_FAR, 0, 0), (PROJECT_HERE, 0, 0),
    (FIRST_PLUS, 2, 0), (FROM_PLUS, 1, 1), (FIRST_MINUS, 2, 0), (FROM_MINUS, 0, 0),
    (FROM_PLUS, 0, 0), (FROM_PLUS, 0, 3), (TRANSPOSE, -1, 3), (FIRST_MINUS, 3, 0),
    (FROM_MINUS, 0, 1), (FIRST_FAR, 1, 0), (FROM_MINUS, 1, 3), (FROM_MINUS, 0, 3),
    (FROM_MINUS, 0, 2), (FIRST_FAR, 2, 0), (TRANSPOSE, -1, 1), (FROM_MINUS, 3, 0),
    (PROJECT_MINUS, 0, 0), (FROM_MINUS, 1, 0), (FROM_PLUS, 0, 2), (FIRST_PLUS, 3, 0),
    (FROM_PLUS, 0, 1), (PROJECT_HERE, 1, 0), (FROM_PLUS, 1, 0), (FROM_PLUS, 2, 1),
    (PROJECT_HERE, 2, 0), (PROJECT_PLUS, 0, 0), (FROM_PLUS, 1, 2), (FROM_PLUS, 3, 3),
    (FROM_MINUS, 3, 3), (FROM_PLUS, 3, 0), (FROM_PLUS, 2, 3), (FROM_MINUS, 2, 0),
    (FROM_MINUS, 1, 2), (FROM_PLUS, 1, 3), (FROM_MINUS, 1, 1), (FROM_MINUS, 2, 3),
    (FROM_MINUS, 2, 1), (PROJECT_MINUS, 1, 0), (FROM_PLUS, 2, 0), (FROM_PLUS, 2, 2),
    (PROJECT_FAR, 0, 0), (GRAD_FAR, 0, 0), (FIRST_FAR, 3, 0), (GRAD_SENT, 0, 0),
    (FROM_MINUS, 2, 2), (PROJECT_MINUS, 2, 0), (PROJECT_PLUS, 2, 0), (PROJECT_HERE, 3, 0),
    (PROJECT_PLUS, 1, 0), (PROJECT_FAR, 2, 0), (GRAD_FAR, 2, 0), (GRAD_RELAYED, 0, 0),
    (FROM_MINUS, 3, 1), (RELAY, 0, 2), (PROJECT_FAR, 1, 0), (GRAD_FAR, 1, 0),
    (GRAD_SENT, 2, 0), (FROM_MINUS, 3, 2), (FROM_PLUS, 3, 2), (GRAD_RELAYED, 2, 0),
    (PROJECT_MINUS, 3, 0), (RELAY, 0, 1), (GRAD_HERE, 0, 0), (GRAD_SENT, 1, 0),
    (GRAD_RELAYED, 1, 0), (RELAY, 2, 3), (RELAY, 1, 2), (FROM_PLUS, 3, 1),
    (RELAY, 0, 3), (PROJECT_PLUS, 3, 0), (SECOND, 0, 2), (RELAY, 1, 1),
    (RELAY, 2, 1), (PROJECT_FAR, 3, 0), (RELAY, 2, 2), (RELAY, 2, 0),
    (GRAD_FAR, 3, 0), (SECOND, 0, 1), (GRAD_HERE, 2, 0), (RELAY, 0, 0),
    (GRAD_SENT, 3, 0), (GRAD_RELAYED, 3, 0), (RELAY, 3, 2), (RELAY, 1, 3),
    (GRAD_HERE, 1, 0), (SECOND, 1, 2), (RELAY, 1, 0), (GRAD_HERE, 3, 0),
    (SECOND, 0, 3), (FAR_PLUS, 0, 0), (FAR_MINUS, 0, 0), (SECOND, 0, 0),
    (RELAY, 3, 1), (SECOND, 1, 1), (SECOND, 2, 2), (RELAY, 3, 3),
    (SECOND, 3, 2), (SECOND, 2, 0), (RELAY, 3, 0), (SECOND, 1, 3),
    (FAR_MINUS, 1, 0), (FAR_PLUS, 1, 0), (SECOND, 2, 3), (SECOND, 2, 1),
    (SECOND, 1, 0), (FINISH, 0, 0), (SECOND, 3, 3), (SECOND, 3, 1),
    (FAR_MINUS, 2, 0), (FAR_PLUS, 3, 0), (FAR_MINUS, 3, 0), (FAR_PLUS, 2, 0),
    (FINISH, 1, 0), (FINISH, 2, 0), (SECOND, 3, 0), (FINISH, 3, 0),
)


def kernel(
    bit,
    act,
    tgt,
    wgt,
    lens,
    out,
    a_v,
    at_v,
    t_v,
    wm,
    wp,
    w_all,
    keys,
    res,
    relay_out,
    relay_in,
    relay_own,
    fin_out_p,
    fin_out_m,
    fin_in_p,
    fin_in_m,
    own1,
    s2_out,
    s2_rin,
    f2_out_p,
    f2_out_m,
    f2_in_p,
    f2_in_m,
    g,
    g_low,
    gp,
    ss,
    ss_all,
    load_sem,
    ag_s,
    ag_r,
    rs_s,
    rs_r,
    y_s,
    y_r,
    ps_s,
    ps_r,
):
    members, tokens, rows = a_v.shape[0], act.shape[0], a_v.shape[2]
    depth = act.shape[1]
    chunks = w_all.shape[0]
    half = rows // 2
    sequences = tokens // SLOT
    fs = lax.axis_index("fsdp")
    rep = lax.axis_index("replica")
    x = lax.div(fs, SIDE)
    z = lax.rem(fs, SIDE)
    mask = 2**bit
    partner = rep + mask - 2 * mask * lax.rem(lax.div(rep, mask), 2)

    def step(v, k):
        return lax.rem(v + k, SIDE)

    def member(c, df, ds):
        if FIRST[c] == "z":
            return step(x, ds) * SIDE + step(z, df)
        return step(x, df) * SIDE + step(z, ds)

    def cut(c):
        return pl.ds(c * LANES, LANES)

    load_w = []
    for c in sorted(range(chunks), key=[o[1] for o in ORDER if o[0] == START].index):
        load_w.append(
            pltpu.make_async_copy(wgt.at[:, cut(c)], wm.at[:, cut(c)], load_sem.at[members + 1 + c])
        )
        load_w[-1].start()
    barrier = pltpu.get_barrier_semaphore()
    peer_y = {"replica": partner}
    for peer in (
        {"fsdp": step(x, 1) * SIDE + z},
        {"fsdp": step(x, 3) * SIDE + z},
        {"fsdp": x * SIDE + step(z, 1)},
        {"fsdp": x * SIDE + step(z, 3)},
        peer_y,
    ):
        pl.semaphore_signal(barrier, inc=1, device_id=peer, device_id_type=MESH)
    load_a = []
    for m in range(members):
        load_a.append(
            pltpu.make_async_copy(
                act.at[:, pl.ds(m * rows, rows)],
                a_v.at[m, pl.ds(0, tokens), :],
                load_sem.at[m],
            )
        )
        load_a[-1].start()
    load_t = pltpu.make_async_copy(tgt, t_v, load_sem.at[members])
    load_t.start()
    for c in range(chunks):
        load_w[c].wait()
    for c in range(chunks):
        w_all[c, fs] = wm[:, cut(c)].astype(jnp.bfloat16)
    pl.semaphore_wait(barrier, 5)

    sent = []

    def send(src, dst, send_sem, recv_sem, to):
        copy = pltpu.make_async_remote_copy(
            src_ref=src,
            dst_ref=dst,
            send_sem=send_sem,
            recv_sem=recv_sem,
            device_id=to,
            device_id_type=MESH,
        )
        copy.start()
        sent.append(copy)

    def arrived(dst, send_sem, recv_sem, to):
        pltpu.make_async_remote_copy(
            src_ref=dst,
            dst_ref=dst,
            send_sem=send_sem,
            recv_sem=recv_sem,
            device_id=to,
            device_id_type=MESH,
        ).wait_recv()

    def to_f(c, k):
        return {"fsdp": member(c, k, 0)}

    def to_s(c, k):
        return {"fsdp": member(c, 0, k)}

    def spread(c, j):
        block = w_all.at[c, member(c, j, 0)]
        send(block, block, ag_s.at[c, 4 + j], ag_r.at[c, 4 + j], to_s(c, 1))
        send(block, block, ag_s.at[c, 8 + j], ag_r.at[c, 8 + j], to_s(c, 3))

    def start(c, _):
        block = w_all.at[c, fs]
        send(block, block, ag_s.at[c, 0], ag_r.at[c, 0], to_f(c, 1))
        send(block, block, ag_s.at[c, 1], ag_r.at[c, 1], to_f(c, 3))
        spread(c, 0)

    def first_minus(c, _):
        block = w_all.at[c, member(c, 3, 0)]
        arrived(block, ag_s.at[c, 0], ag_r.at[c, 0], to_f(c, 1))
        part = block.at[pl.ds(0, half), :]
        send(part, part, ag_s.at[c, 2], ag_r.at[c, 2], to_f(c, 1))
        spread(c, 3)

    def first_plus(c, _):
        block = w_all.at[c, member(c, 1, 0)]
        arrived(block, ag_s.at[c, 1], ag_r.at[c, 1], to_f(c, 3))
        part = block.at[pl.ds(half, half), :]
        send(part, part, ag_s.at[c, 3], ag_r.at[c, 3], to_f(c, 3))
        spread(c, 1)

    def first_far(c, _):
        block = w_all.at[c, member(c, 2, 0)]
        arrived(block.at[pl.ds(0, half), :], ag_s.at[c, 2], ag_r.at[c, 2], to_f(c, 1))
        arrived(block.at[pl.ds(half, half), :], ag_s.at[c, 3], ag_r.at[c, 3], to_f(c, 3))
        spread(c, 2)

    def from_minus(c, j):
        block = w_all.at[c, member(c, j, 3)]
        arrived(block, ag_s.at[c, 4 + j], ag_r.at[c, 4 + j], to_s(c, 1))
        if j < 2:
            send(block, block, ag_s.at[c, 12 + j], ag_r.at[c, 12 + j], to_s(c, 1))

    def from_plus(c, j):
        block = w_all.at[c, member(c, j, 1)]
        arrived(block, ag_s.at[c, 8 + j], ag_r.at[c, 8 + j], to_s(c, 3))
        if j >= 2:
            send(block, block, ag_s.at[c, 12 + j], ag_r.at[c, 12 + j], to_s(c, 3))

    def project(c, ds, fresh=False):
        def body(j, carry):
            m = member(c, j, ds)
            keys[c] += jnp.dot(
                a_v[m, pl.ds(0, tokens), :], w_all[c, m], preferred_element_type=jnp.float32
            )
            return carry

        if fresh:
            keys[c] = jnp.zeros((tokens, LANES), jnp.float32)
        lax.fori_loop(0, SIDE, body, 0)

    def project_here(c, _):
        if not loaded:
            load_all()
        project(c, 0, fresh=True)

    def project_minus(c, _):
        project(c, 3)

    def project_plus(c, _):
        project(c, 1)

    def project_far(c, _):
        for j in range(SIDE):
            block = w_all.at[c, member(c, j, 2)]
            arrived(block, ag_s.at[c, 12 + j], ag_r.at[c, 12 + j], to_s(c, 1 if j < 2 else 3))
        project(c, 2)

    loaded = []

    def load_all():
        for copy in load_a:
            copy.wait()
        load_t.wait()
        pad = a_v.shape[1] - tokens
        if pad:
            for c in range(chunks):
                res[c, pl.ds(tokens, pad), :] = jnp.zeros((pad, LANES), res.dtype)
            for m in range(members):
                a_v[m, pl.ds(tokens, pad), :] = jnp.zeros((pad, rows), a_v.dtype)
        loaded.append(True)

    def transpose(_, k):
        def body(m, carry):
            at_v[m] = a_v[m].T
            return carry

        if not loaded:
            load_all()
        lax.fori_loop(k * (members // 4), (k + 1) * (members // 4), body, 0)

    def times_residual(c, j, ds):
        return jnp.dot(at_v[member(c, j, ds)], res[c], preferred_element_type=jnp.float32)

    def grad_far(c, _):
        for k in range(sequences):
            span = pl.ds(k * SLOT, SLOT)
            live = lax.broadcasted_iota(jnp.int32, (SLOT, LANES), 0) < lens[fs * sequences + k]
            wanted = t_v[span, c * LANES : (c + 1) * LANES].astype(jnp.float32)
            keys_out = keys[c, span, :] * depth ** (-0.5)
            res[c, span, :] = jnp.where(live, keys_out - wanted, 0.0).astype(jnp.bfloat16)

        def far(j, carry):
            relay_out[c, j] = times_residual(c, j, 2).astype(jnp.bfloat16)
            return carry

        lax.fori_loop(0, SIDE, far, 0)
        for j in range(SIDE):
            send(
                relay_out.at[c, j],
                relay_in.at[c, j],
                rs_s.at[c, j],
                rs_r.at[c, j],
                to_s(c, 1 if j < 2 else 3),
            )

    def grad_sent(c, _):
        def plus(j, carry):
            fin_out_p[c, j] = times_residual(c, j, 1).astype(jnp.bfloat16)
            return carry

        def minus(j, carry):
            fin_out_m[c, j] = times_residual(c, j, 3).astype(jnp.bfloat16)
            return carry

        lax.fori_loop(2, SIDE, plus, 0)
        for j in (2, 3):
            send_plus(c, j)
        lax.fori_loop(0, 2, minus, 0)
        for j in (0, 1):
            send_minus(c, j)

    def grad_relayed(c, _):
        def plus(j, carry):
            relay_own[c, j] = times_residual(c, j, 1)
            return carry

        def minus(j, carry):
            relay_own[c, j] = times_residual(c, j, 3)
            return carry

        lax.fori_loop(0, 2, plus, 0)
        lax.fori_loop(2, SIDE, minus, 0)

    def grad_here(c, _):
        def body(j, carry):
            own1[c, j] = times_residual(c, j, 0)
            return carry

        lax.fori_loop(0, SIDE, body, 0)

    def send_plus(c, j):
        send(
            fin_out_p.at[c, j], fin_in_m.at[c, j], rs_s.at[c, 4 + j], rs_r.at[c, 4 + j], to_s(c, 1)
        )

    def send_minus(c, j):
        send(
            fin_out_m.at[c, j], fin_in_p.at[c, j], rs_s.at[c, 8 + j], rs_r.at[c, 8 + j], to_s(c, 3)
        )

    def relay(c, j):
        arrived(relay_in.at[c, j], rs_s.at[c, j], rs_r.at[c, j], to_s(c, 1 if j < 2 else 3))
        total = (relay_own[c, j] + relay_in[c, j].astype(jnp.float32)).astype(jnp.bfloat16)
        if j < 2:
            fin_out_p[c, j] = total
            send_plus(c, j)
        else:
            fin_out_m[c, j] = total
            send_minus(c, j)

    def second(c, j):
        arrived(fin_in_m.at[c, j], rs_s.at[c, 4 + j], rs_r.at[c, 4 + j], to_s(c, 1))
        arrived(fin_in_p.at[c, j], rs_s.at[c, 8 + j], rs_r.at[c, 8 + j], to_s(c, 3))
        total = (
            own1[c, j] + fin_in_m[c, j].astype(jnp.float32) + fin_in_p[c, j].astype(jnp.float32)
        )
        if j != 2:
            own1[c, j] = total
            return
        s2_out[c] = total.astype(jnp.bfloat16)
        for k, to in ((0, 1), (1, 3)):
            send(
                s2_out.at[c, pl.ds(k * half, half), :],
                s2_rin.at[c, k],
                rs_s.at[c, 12 + k],
                rs_r.at[c, 12 + k],
                to_f(c, to),
            )

    upper, lower = pl.ds(0, half), pl.ds(half, half)

    def far_minus(c, _):
        arrived(s2_rin.at[c, 0], rs_s.at[c, 12], rs_r.at[c, 12], to_f(c, 1))
        f2_out_p[c, upper, :] = (
            own1[c, 1, upper, :] + s2_rin[c, 0].astype(jnp.float32)
        ).astype(jnp.bfloat16)
        f2_out_p[c, lower, :] = own1[c, 1, lower, :].astype(jnp.bfloat16)
        send(f2_out_p.at[c], f2_in_m.at[c], rs_s.at[c, 14], rs_r.at[c, 14], to_f(c, 1))

    def far_plus(c, _):
        arrived(s2_rin.at[c, 1], rs_s.at[c, 13], rs_r.at[c, 13], to_f(c, 3))
        f2_out_m[c, lower, :] = (
            own1[c, 3, lower, :] + s2_rin[c, 1].astype(jnp.float32)
        ).astype(jnp.bfloat16)
        f2_out_m[c, upper, :] = own1[c, 3, upper, :].astype(jnp.bfloat16)
        send(f2_out_m.at[c], f2_in_p.at[c], rs_s.at[c, 15], rs_r.at[c, 15], to_f(c, 3))

    done = []

    def finish(c, _):
        arrived(f2_in_m.at[c], rs_s.at[c, 14], rs_r.at[c, 14], to_f(c, 1))
        arrived(f2_in_p.at[c], rs_s.at[c, 15], rs_r.at[c, 15], to_f(c, 3))
        total = own1[c, 0] + f2_in_m[c].astype(jnp.float32) + f2_in_p[c].astype(jnp.float32)
        g[c] = total
        g_low[c] = total.astype(jnp.bfloat16)
        squares = jnp.sum((total * total).reshape(rows // 8, 8, LANES), axis=0)
        done.append(c)
        if len(done) > 1:
            squares += ss[...]
        ss[...] = squares
        if len(done) == chunks:
            share_squares()
        send(g_low.at[c], gp.at[c], y_s.at[c], y_r.at[c], peer_y)

    def share_squares():
        arrived(wp, y_s.at[chunks], y_r.at[chunks], peer_y)
        arrived(gp.at[done[0]], y_s.at[done[0]], y_r.at[done[0]], peer_y)
        ss_all[0, fs] = jnp.sum(ss[...], axis=0, keepdims=True)
        own = ss_all.at[0, fs]
        for k in range(members):
            to = {"replica": partner, "fsdp": lax.rem(fs + k, members)}
            send(own, ss_all.at[1, fs], ps_s.at[1, k], ps_r.at[1, fs], to)
        for k in range(1, members):
            to = {"fsdp": lax.rem(fs + k, members)}
            send(own, ss_all.at[0, fs], ps_s.at[0, k], ps_r.at[0, fs], to)

    steps = {
        START: start,
        FIRST_MINUS: first_minus,
        FIRST_PLUS: first_plus,
        FIRST_FAR: first_far,
        FROM_MINUS: from_minus,
        FROM_PLUS: from_plus,
        PROJECT_HERE: project_here,
        PROJECT_MINUS: project_minus,
        PROJECT_PLUS: project_plus,
        PROJECT_FAR: project_far,
        TRANSPOSE: transpose,
        GRAD_FAR: grad_far,
        GRAD_SENT: grad_sent,
        GRAD_RELAYED: grad_relayed,
        GRAD_HERE: grad_here,
        RELAY: relay,
        SECOND: second,
        FAR_MINUS: far_minus,
        FAR_PLUS: far_plus,
        FINISH: finish,
    }
    starts = 0
    for name, c, which in ORDER:
        steps[name](c, which)
        starts += name == START
        if name == START and starts == 1:
            send(wm, wp, y_s.at[chunks], y_r.at[chunks], peer_y)

    entries = depth * LANES * chunks

    def scale(group):
        total = jnp.sum(ss_all[group], axis=(0, 1, 2), keepdims=True)[0]
        return (0.5 * learning_rate) * lax.rsqrt(total / entries + epsilon)

    for c in range(chunks):
        wp[:, cut(c)] = 0.5 * (wm[:, cut(c)] + wp[:, cut(c)])
    for k in range(1, members):
        m = lax.rem(fs + k, members)
        arrived(ss_all.at[0, m], ps_s.at[0, k], ps_r.at[0, m], peer_y)
    own_scale = scale(0)
    for c in done[1:]:
        arrived(gp.at[c], y_s.at[c], y_r.at[c], peer_y)
    for k in range(members):
        m = lax.rem(fs + k, members)
        arrived(ss_all.at[1, m], ps_s.at[1, k], ps_r.at[1, m], peer_y)
    partner_scale = scale(1)
    for c in range(chunks):
        out[:, cut(c)] = wp[:, cut(c)] - own_scale * g[c] - partner_scale * gp[c].astype(jnp.float32)
    for copy in sent:
        copy.wait_send()


def local(activations, targets, weights, lengths):
    tokens, depth = activations.shape[1:]
    rows, columns = weights.shape[1:]
    members = lax.axis_size("fsdp")
    chunks = columns // LANES
    bit = STEP % (lax.axis_size("replica").bit_length() - 1)
    padded = -(-tokens // LANES) * LANES
    bf16, f32 = jnp.bfloat16, jnp.float32
    vmem = pltpu.VMEM
    dma = pltpu.SemaphoreType.DMA
    block = (rows, LANES)
    any_spec = pl.BlockSpec(memory_space=pl.ANY)
    averaged = pl.pallas_call(
        functools.partial(kernel, bit),
        out_shape=jax.ShapeDtypeStruct((rows, columns), f32),
        in_specs=[any_spec, any_spec, any_spec, pl.BlockSpec(memory_space=pltpu.SMEM)],
        out_specs=pl.BlockSpec(memory_space=pltpu.VMEM),
        scratch_shapes=[
            vmem((members, padded, rows), bf16),
            vmem((members, rows, padded), bf16),
            vmem((tokens, columns), bf16),
            vmem((rows, columns), f32),
            vmem((rows, columns), f32),
            vmem((chunks, members) + block, bf16),
            vmem((chunks, tokens, LANES), f32),
            vmem((chunks, padded, LANES), bf16),
            vmem((chunks, SIDE) + block, bf16),
            vmem((chunks, SIDE) + block, bf16),
            vmem((chunks, SIDE) + block, f32),
            vmem((chunks, SIDE) + block, bf16),
            vmem((chunks, SIDE) + block, bf16),
            vmem((chunks, SIDE) + block, bf16),
            vmem((chunks, SIDE) + block, bf16),
            vmem((chunks, SIDE) + block, f32),
            vmem((chunks,) + block, bf16),
            vmem((chunks, 2, rows // 2, LANES), bf16),
            vmem((chunks,) + block, bf16),
            vmem((chunks,) + block, bf16),
            vmem((chunks,) + block, bf16),
            vmem((chunks,) + block, bf16),
            vmem((chunks,) + block, f32),
            vmem((chunks,) + block, bf16),
            vmem((chunks,) + block, bf16),
            vmem((8, LANES), f32),
            vmem((2, members, 1, LANES), f32),
            dma((members + chunks + 1,)),
            dma((chunks, 16)),
            dma((chunks, 16)),
            dma((chunks, 16)),
            dma((chunks, 16)),
            dma((chunks + 1,)),
            dma((chunks + 1,)),
            dma((2, members)),
            dma((2, members)),
        ],
        compiler_params=pltpu.CompilerParams(
            collective_id=0, has_side_effects=True, vmem_limit_bytes=60 * 2**20
        ),
    )(activations[0], targets[0], weights[0], lengths[0])
    return averaged[None]


def solution(mesh):
    return jax.shard_map(
        local,
        mesh=mesh,
        in_specs=(
            P("replica", "fsdp", None),
            P("replica", "fsdp", None),
            P("replica", "fsdp", None),
            P("replica", None),
        ),
        out_specs=P("replica", "fsdp", None),
        check_vma=False,
    )
```

```python
import functools

import jax
import jax.numpy as jnp
from jax import lax
from jax.experimental import pallas as pl
from jax.experimental.pallas import tpu as pltpu
from jax.sharding import PartitionSpec as P

SLOT = 64
STEP = 3
LANES = 128
SIDE = 4

learning_rate = 0.1
epsilon = 1e-06

MESH = pl.DeviceIdType.MESH
FIRST = ("z", "z", "x", "z")
(
    FROM_MINUS,
    FROM_PLUS,
    FIRST_MINUS,
    FIRST_PLUS,
    FIRST_FAR,
    PROJECT_HERE,
    PROJECT_MINUS,
    PROJECT_PLUS,
    PROJECT_FAR,
    GRAD_FAR,
    GRAD_SENT,
    GRAD_RELAYED,
    GRAD_HERE,
    RELAY,
    SECOND,
    FAR_MINUS,
    FAR_PLUS,
    FINISH,
    START,
    TRANSPOSE,
) = range(20)
ORDER = (
    (START, 0, 0), (START, 1, 0), (START, 3, 0), (TRANSPOSE, -1, 2),
    (FIRST_PLUS, 0, 0), (FIRST_MINUS, 0, 0), (START, 2, 0), (FIRST_MINUS, 1, 0),
    (TRANSPOSE, -1, 0), (FIRST_PLUS, 1, 0), (FIRST_FAR, 0, 0), (PROJECT_HERE, 0, 0),
    (FIRST_PLUS, 2, 0), (FROM_PLUS, 1, 1), (FIRST_MINUS, 2, 0), (FROM_MINUS, 0, 0),
    (FROM_PLUS, 0, 0), (FROM_PLUS, 0, 3), (TRANSPOSE, -1, 3), (FIRST_MINUS, 3, 0),
    (FROM_MINUS, 0, 1), (FIRST_FAR, 1, 0), (FROM_MINUS, 1, 3), (FROM_MINUS, 0, 3),
    (FROM_MINUS, 0, 2), (FIRST_FAR, 2, 0), (TRANSPOSE, -1, 1), (FROM_MINUS, 3, 0),
    (PROJECT_MINUS, 0, 0), (FROM_MINUS, 1, 0), (FROM_PLUS, 0, 2), (FIRST_PLUS, 3, 0),
    (FROM_PLUS, 0, 1), (PROJECT_HERE, 1, 0), (FROM_PLUS, 1, 0), (FROM_PLUS, 2, 1),
    (PROJECT_HERE, 2, 0), (PROJECT_PLUS, 0, 0), (FROM_PLUS, 1, 2), (FROM_PLUS, 3, 3),
    (FROM_MINUS, 3, 3), (FROM_PLUS, 3, 0), (FROM_PLUS, 2, 3), (FROM_MINUS, 2, 0),
    (FROM_MINUS, 1, 2), (FROM_PLUS, 1, 3), (FROM_MINUS, 1, 1), (FROM_MINUS, 2, 3),
    (FROM_MINUS, 2, 1), (PROJECT_MINUS, 1, 0), (FROM_PLUS, 2, 0), (FROM_PLUS, 2, 2),
    (PROJECT_FAR, 0, 0), (GRAD_FAR, 0, 0), (FIRST_FAR, 3, 0), (GRAD_SENT, 0, 0),
    (FROM_MINUS, 2, 2), (PROJECT_MINUS, 2, 0), (PROJECT_PLUS, 2, 0), (PROJECT_HERE, 3, 0),
    (PROJECT_PLUS, 1, 0), (PROJECT_FAR, 2, 0), (GRAD_FAR, 2, 0), (GRAD_RELAYED, 0, 0),
    (FROM_MINUS, 3, 1), (RELAY, 0, 2), (PROJECT_FAR, 1, 0), (GRAD_FAR, 1, 0),
    (GRAD_SENT, 2, 0), (FROM_MINUS, 3, 2), (FROM_PLUS, 3, 2), (GRAD_RELAYED, 2, 0),
    (PROJECT_MINUS, 3, 0), (RELAY, 0, 1), (GRAD_HERE, 0, 0), (GRAD_SENT, 1, 0),
    (GRAD_RELAYED, 1, 0), (RELAY, 2, 3), (RELAY, 1, 2), (FROM_PLUS, 3, 1),
    (RELAY, 0, 3), (PROJECT_PLUS, 3, 0), (SECOND, 0, 2), (RELAY, 1, 1),
    (RELAY, 2, 1), (PROJECT_FAR, 3, 0), (RELAY, 2, 2), (RELAY, 2, 0),
    (GRAD_FAR, 3, 0), (SECOND, 0, 1), (GRAD_HERE, 2, 0), (RELAY, 0, 0),
    (GRAD_SENT, 3, 0), (GRAD_RELAYED, 3, 0), (RELAY, 3, 2), (RELAY, 1, 3),
    (GRAD_HERE, 1, 0), (SECOND, 1, 2), (RELAY, 1, 0), (GRAD_HERE, 3, 0),
    (SECOND, 0, 3), (FAR_PLUS, 0, 0), (FAR_MINUS, 0, 0), (SECOND, 0, 0),
    (RELAY, 3, 1), (SECOND, 1, 1), (SECOND, 2, 2), (RELAY, 3, 3),
    (SECOND, 3, 2), (SECOND, 2, 0), (RELAY, 3, 0), (SECOND, 1, 3),
    (FAR_MINUS, 1, 0), (FAR_PLUS, 1, 0), (SECOND, 2, 3), (SECOND, 2, 1),
    (SECOND, 1, 0), (FINISH, 0, 0), (SECOND, 3, 3), (SECOND, 3, 1),
    (FAR_MINUS, 2, 0), (FAR_PLUS, 3, 0), (FAR_MINUS, 3, 0), (FAR_PLUS, 2, 0),
    (FINISH, 1, 0), (FINISH, 2, 0), (SECOND, 3, 0), (FINISH, 3, 0),
)


def kernel(
    bit,
    act,
    tgt,
    wgt,
    lens,
    out,
    a_v,
    at_v,
    t_v,
    wm,
    wp,
    w_all,
    keys,
    res,
    relay_out,
    relay_in,
    relay_own,
    fin_out_p,
    fin_out_m,
    fin_in_p,
    fin_in_m,
    own1,
    s2_out,
    s2_rin,
    f2_out_p,
    f2_out_m,
    f2_in_p,
    f2_in_m,
    g,
    g_low,
    gp,
    ss,
    ss_all,
    load_sem,
    ag_s,
    ag_r,
    rs_s,
    rs_r,
    y_s,
    y_r,
    ps_s,
    ps_r,
):
    members, tokens, rows = a_v.shape[0], act.shape[0], a_v.shape[2]
    depth = act.shape[1]
    chunks = w_all.shape[0]
    half = rows // 2
    sequences = tokens // SLOT
    fs = lax.axis_index("fsdp")
    rep = lax.axis_index("replica")
    x = lax.div(fs, SIDE)
    z = lax.rem(fs, SIDE)
    mask = 2**bit
    partner = rep + mask - 2 * mask * lax.rem(lax.div(rep, mask), 2)

    def step(v, k):
        return lax.rem(v + k, SIDE)

    def member(c, df, ds):
        if FIRST[c] == "z":
            return step(x, ds) * SIDE + step(z, df)
        return step(x, df) * SIDE + step(z, ds)

    def cut(c):
        return pl.ds(c * LANES, LANES)

    barrier = pltpu.get_barrier_semaphore()
    peer_y = {"replica": partner}
    for peer in (
        {"fsdp": step(x, 1) * SIDE + z},
        {"fsdp": step(x, 3) * SIDE + z},
        {"fsdp": x * SIDE + step(z, 1)},
        {"fsdp": x * SIDE + step(z, 3)},
        peer_y,
    ):
        pl.semaphore_signal(barrier, inc=1, device_id=peer, device_id_type=MESH)
    load_w = {}
    for c in sorted(range(chunks), key=[o[1] for o in ORDER if o[0] == START].index):
        load_w[c] = pltpu.make_async_copy(
            wgt.at[:, cut(c)], wm.at[:, cut(c)], load_sem.at[members + 1 + c]
        )
        load_w[c].start()
    load_a = []
    for m in range(members):
        load_a.append(
            pltpu.make_async_copy(
                act.at[:, pl.ds(m * rows, rows)],
                a_v.at[m, pl.ds(0, tokens), :],
                load_sem.at[m],
            )
        )
        load_a[-1].start()
    load_t = pltpu.make_async_copy(tgt, t_v, load_sem.at[members])
    load_t.start()

    def round_rows(c):
        load_w[c].wait()
        w_all[c, fs] = wm[:, cut(c)].astype(jnp.bfloat16)

    round_rows(ORDER[0][1])
    pl.semaphore_wait(barrier, 5)

    sent = []

    def send(src, dst, send_sem, recv_sem, to):
        copy = pltpu.make_async_remote_copy(
            src_ref=src,
            dst_ref=dst,
            send_sem=send_sem,
            recv_sem=recv_sem,
            device_id=to,
            device_id_type=MESH,
        )
        copy.start()
        sent.append(copy)

    def arrived(dst, send_sem, recv_sem, to):
        pltpu.make_async_remote_copy(
            src_ref=dst,
            dst_ref=dst,
            send_sem=send_sem,
            recv_sem=recv_sem,
            device_id=to,
            device_id_type=MESH,
        ).wait_recv()

    def to_f(c, k):
        return {"fsdp": member(c, k, 0)}

    def to_s(c, k):
        return {"fsdp": member(c, 0, k)}

    def spread(c, j):
        block = w_all.at[c, member(c, j, 0)]
        send(block, block, ag_s.at[c, 4 + j], ag_r.at[c, 4 + j], to_s(c, 1))
        send(block, block, ag_s.at[c, 8 + j], ag_r.at[c, 8 + j], to_s(c, 3))

    def start(c, _):
        block = w_all.at[c, fs]
        send(block, block, ag_s.at[c, 0], ag_r.at[c, 0], to_f(c, 1))
        send(block, block, ag_s.at[c, 1], ag_r.at[c, 1], to_f(c, 3))
        spread(c, 0)

    def first_minus(c, _):
        block = w_all.at[c, member(c, 3, 0)]
        arrived(block, ag_s.at[c, 0], ag_r.at[c, 0], to_f(c, 1))
        part = block.at[pl.ds(0, half), :]
        send(part, part, ag_s.at[c, 2], ag_r.at[c, 2], to_f(c, 1))
        spread(c, 3)

    def first_plus(c, _):
        block = w_all.at[c, member(c, 1, 0)]
        arrived(block, ag_s.at[c, 1], ag_r.at[c, 1], to_f(c, 3))
        part = block.at[pl.ds(half, half), :]
        send(part, part, ag_s.at[c, 3], ag_r.at[c, 3], to_f(c, 3))
        spread(c, 1)

    def first_far(c, _):
        block = w_all.at[c, member(c, 2, 0)]
        arrived(block.at[pl.ds(0, half), :], ag_s.at[c, 2], ag_r.at[c, 2], to_f(c, 1))
        arrived(block.at[pl.ds(half, half), :], ag_s.at[c, 3], ag_r.at[c, 3], to_f(c, 3))
        spread(c, 2)

    def from_minus(c, j):
        block = w_all.at[c, member(c, j, 3)]
        arrived(block, ag_s.at[c, 4 + j], ag_r.at[c, 4 + j], to_s(c, 1))
        if j < 2:
            send(block, block, ag_s.at[c, 12 + j], ag_r.at[c, 12 + j], to_s(c, 1))

    def from_plus(c, j):
        block = w_all.at[c, member(c, j, 1)]
        arrived(block, ag_s.at[c, 8 + j], ag_r.at[c, 8 + j], to_s(c, 3))
        if j >= 2:
            send(block, block, ag_s.at[c, 12 + j], ag_r.at[c, 12 + j], to_s(c, 3))

    def project(c, ds, fresh=False):
        def body(j, carry):
            m = member(c, j, ds)
            keys[c] += jnp.dot(
                a_v[m, pl.ds(0, tokens), :], w_all[c, m], preferred_element_type=jnp.float32
            )
            return carry

        if fresh:
            keys[c] = jnp.zeros((tokens, LANES), jnp.float32)
        lax.fori_loop(0, SIDE, body, 0)

    def project_here(c, _):
        if not loaded:
            load_all()
        project(c, 0, fresh=True)

    def project_minus(c, _):
        project(c, 3)

    def project_plus(c, _):
        project(c, 1)

    def project_far(c, _):
        for j in range(SIDE):
            block = w_all.at[c, member(c, j, 2)]
            arrived(block, ag_s.at[c, 12 + j], ag_r.at[c, 12 + j], to_s(c, 1 if j < 2 else 3))
        project(c, 2)

    loaded = []

    def load_all():
        for copy in load_a:
            copy.wait()
        load_t.wait()
        pad = a_v.shape[1] - tokens
        if pad:
            for c in range(chunks):
                res[c, pl.ds(tokens, pad), :] = jnp.zeros((pad, LANES), res.dtype)
            for m in range(members):
                a_v[m, pl.ds(tokens, pad), :] = jnp.zeros((pad, rows), a_v.dtype)
        loaded.append(True)

    def transpose(_, k):
        def body(m, carry):
            at_v[m] = a_v[m].T
            return carry

        if not loaded:
            load_all()
        lax.fori_loop(k * (members // 4), (k + 1) * (members // 4), body, 0)

    def times_residual(c, j, ds):
        return jnp.dot(at_v[member(c, j, ds)], res[c], preferred_element_type=jnp.float32)

    def grad_far(c, _):
        for k in range(sequences):
            span = pl.ds(k * SLOT, SLOT)
            live = lax.broadcasted_iota(jnp.int32, (SLOT, LANES), 0) < lens[fs * sequences + k]
            wanted = t_v[span, c * LANES : (c + 1) * LANES].astype(jnp.float32)
            keys_out = keys[c, span, :] * depth ** (-0.5)
            res[c, span, :] = jnp.where(live, keys_out - wanted, 0.0).astype(jnp.bfloat16)

        def far(j, carry):
            relay_out[c, j] = times_residual(c, j, 2).astype(jnp.bfloat16)
            return carry

        lax.fori_loop(0, SIDE, far, 0)
        for j in range(SIDE):
            send(
                relay_out.at[c, j],
                relay_in.at[c, j],
                rs_s.at[c, j],
                rs_r.at[c, j],
                to_s(c, 1 if j < 2 else 3),
            )

    def grad_sent(c, _):
        def plus(j, carry):
            fin_out_p[c, j] = times_residual(c, j, 1).astype(jnp.bfloat16)
            return carry

        def minus(j, carry):
            fin_out_m[c, j] = times_residual(c, j, 3).astype(jnp.bfloat16)
            return carry

        lax.fori_loop(2, SIDE, plus, 0)
        for j in (2, 3):
            send_plus(c, j)
        lax.fori_loop(0, 2, minus, 0)
        for j in (0, 1):
            send_minus(c, j)

    def grad_relayed(c, _):
        def plus(j, carry):
            relay_own[c, j] = times_residual(c, j, 1)
            return carry

        def minus(j, carry):
            relay_own[c, j] = times_residual(c, j, 3)
            return carry

        lax.fori_loop(0, 2, plus, 0)
        lax.fori_loop(2, SIDE, minus, 0)

    def grad_here(c, _):
        def body(j, carry):
            own1[c, j] = times_residual(c, j, 0)
            return carry

        lax.fori_loop(0, SIDE, body, 0)

    def send_plus(c, j):
        send(
            fin_out_p.at[c, j], fin_in_m.at[c, j], rs_s.at[c, 4 + j], rs_r.at[c, 4 + j], to_s(c, 1)
        )

    def send_minus(c, j):
        send(
            fin_out_m.at[c, j], fin_in_p.at[c, j], rs_s.at[c, 8 + j], rs_r.at[c, 8 + j], to_s(c, 3)
        )

    def relay(c, j):
        arrived(relay_in.at[c, j], rs_s.at[c, j], rs_r.at[c, j], to_s(c, 1 if j < 2 else 3))
        total = (relay_own[c, j] + relay_in[c, j].astype(jnp.float32)).astype(jnp.bfloat16)
        if j < 2:
            fin_out_p[c, j] = total
            send_plus(c, j)
        else:
            fin_out_m[c, j] = total
            send_minus(c, j)

    def second(c, j):
        arrived(fin_in_m.at[c, j], rs_s.at[c, 4 + j], rs_r.at[c, 4 + j], to_s(c, 1))
        arrived(fin_in_p.at[c, j], rs_s.at[c, 8 + j], rs_r.at[c, 8 + j], to_s(c, 3))
        total = (
            own1[c, j] + fin_in_m[c, j].astype(jnp.float32) + fin_in_p[c, j].astype(jnp.float32)
        )
        if j != 2:
            own1[c, j] = total
            return
        s2_out[c] = total.astype(jnp.bfloat16)
        for k, to in ((0, 1), (1, 3)):
            send(
                s2_out.at[c, pl.ds(k * half, half), :],
                s2_rin.at[c, k],
                rs_s.at[c, 12 + k],
                rs_r.at[c, 12 + k],
                to_f(c, to),
            )

    upper, lower = pl.ds(0, half), pl.ds(half, half)

    def far_minus(c, _):
        arrived(s2_rin.at[c, 0], rs_s.at[c, 12], rs_r.at[c, 12], to_f(c, 1))
        f2_out_p[c, upper, :] = (
            own1[c, 1, upper, :] + s2_rin[c, 0].astype(jnp.float32)
        ).astype(jnp.bfloat16)
        f2_out_p[c, lower, :] = own1[c, 1, lower, :].astype(jnp.bfloat16)
        send(f2_out_p.at[c], f2_in_m.at[c], rs_s.at[c, 14], rs_r.at[c, 14], to_f(c, 1))

    def far_plus(c, _):
        arrived(s2_rin.at[c, 1], rs_s.at[c, 13], rs_r.at[c, 13], to_f(c, 3))
        f2_out_m[c, lower, :] = (
            own1[c, 3, lower, :] + s2_rin[c, 1].astype(jnp.float32)
        ).astype(jnp.bfloat16)
        f2_out_m[c, upper, :] = own1[c, 3, upper, :].astype(jnp.bfloat16)
        send(f2_out_m.at[c], f2_in_p.at[c], rs_s.at[c, 15], rs_r.at[c, 15], to_f(c, 3))

    done = []

    def finish(c, _):
        arrived(f2_in_m.at[c], rs_s.at[c, 14], rs_r.at[c, 14], to_f(c, 1))
        arrived(f2_in_p.at[c], rs_s.at[c, 15], rs_r.at[c, 15], to_f(c, 3))
        total = own1[c, 0] + f2_in_m[c].astype(jnp.float32) + f2_in_p[c].astype(jnp.float32)
        g[c] = total
        g_low[c] = total.astype(jnp.bfloat16)
        squares = jnp.sum((total * total).reshape(rows // 8, 8, LANES), axis=0)
        done.append(c)
        if len(done) > 1:
            squares += ss[...]
        ss[...] = squares
        if len(done) == chunks:
            share_squares()
        send(g_low.at[c], gp.at[c], y_s.at[c], y_r.at[c], peer_y)

    def share_squares():
        arrived(wp, y_s.at[chunks], y_r.at[chunks], peer_y)
        arrived(gp.at[done[0]], y_s.at[done[0]], y_r.at[done[0]], peer_y)
        ss_all[0, fs] = jnp.sum(ss[...], axis=0, keepdims=True)
        own = ss_all.at[0, fs]
        for k in range(members):
            to = {"replica": partner, "fsdp": lax.rem(fs + k, members)}
            send(own, ss_all.at[1, fs], ps_s.at[1, k], ps_r.at[1, fs], to)
        for k in range(1, members):
            to = {"fsdp": lax.rem(fs + k, members)}
            send(own, ss_all.at[0, fs], ps_s.at[0, k], ps_r.at[0, fs], to)

    steps = {
        START: start,
        FIRST_MINUS: first_minus,
        FIRST_PLUS: first_plus,
        FIRST_FAR: first_far,
        FROM_MINUS: from_minus,
        FROM_PLUS: from_plus,
        PROJECT_HERE: project_here,
        PROJECT_MINUS: project_minus,
        PROJECT_PLUS: project_plus,
        PROJECT_FAR: project_far,
        TRANSPOSE: transpose,
        GRAD_FAR: grad_far,
        GRAD_SENT: grad_sent,
        GRAD_RELAYED: grad_relayed,
        GRAD_HERE: grad_here,
        RELAY: relay,
        SECOND: second,
        FAR_MINUS: far_minus,
        FAR_PLUS: far_plus,
        FINISH: finish,
    }
    starts = 0
    for name, c, which in ORDER:
        steps[name](c, which)
        starts += name == START
        if name == START and starts == 1:
            for other in range(chunks):
                if other != c:
                    round_rows(other)
            send(wm, wp, y_s.at[chunks], y_r.at[chunks], peer_y)

    entries = depth * LANES * chunks

    def scale(group):
        total = jnp.sum(ss_all[group], axis=(0, 1, 2), keepdims=True)[0]
        return (0.5 * learning_rate) * lax.rsqrt(total / entries + epsilon)

    for c in range(chunks):
        wp[:, cut(c)] = 0.5 * (wm[:, cut(c)] + wp[:, cut(c)])
    for k in range(1, members):
        m = lax.rem(fs + k, members)
        arrived(ss_all.at[0, m], ps_s.at[0, k], ps_r.at[0, m], peer_y)
    own_scale = scale(0)
    for c in done[1:]:
        arrived(gp.at[c], y_s.at[c], y_r.at[c], peer_y)
    for k in range(members):
        m = lax.rem(fs + k, members)
        arrived(ss_all.at[1, m], ps_s.at[1, k], ps_r.at[1, m], peer_y)
    partner_scale = scale(1)
    for c in range(chunks):
        out[:, cut(c)] = wp[:, cut(c)] - own_scale * g[c] - partner_scale * gp[c].astype(jnp.float32)
    for copy in sent:
        copy.wait_send()


def local(activations, targets, weights, lengths):
    tokens, depth = activations.shape[1:]
    rows, columns = weights.shape[1:]
    members = lax.axis_size("fsdp")
    chunks = columns // LANES
    bit = STEP % (lax.axis_size("replica").bit_length() - 1)
    padded = -(-tokens // LANES) * LANES
    bf16, f32 = jnp.bfloat16, jnp.float32
    vmem = pltpu.VMEM
    dma = pltpu.SemaphoreType.DMA
    block = (rows, LANES)
    any_spec = pl.BlockSpec(memory_space=pl.ANY)
    averaged = pl.pallas_call(
        functools.partial(kernel, bit),
        out_shape=jax.ShapeDtypeStruct((rows, columns), f32),
        in_specs=[any_spec, any_spec, any_spec, pl.BlockSpec(memory_space=pltpu.SMEM)],
        out_specs=pl.BlockSpec(memory_space=pltpu.VMEM),
        scratch_shapes=[
            vmem((members, padded, rows), bf16),
            vmem((members, rows, padded), bf16),
            vmem((tokens, columns), bf16),
            vmem((rows, columns), f32),
            vmem((rows, columns), f32),
            vmem((chunks, members) + block, bf16),
            vmem((chunks, tokens, LANES), f32),
            vmem((chunks, padded, LANES), bf16),
            vmem((chunks, SIDE) + block, bf16),
            vmem((chunks, SIDE) + block, bf16),
            vmem((chunks, SIDE) + block, f32),
            vmem((chunks, SIDE) + block, bf16),
            vmem((chunks, SIDE) + block, bf16),
            vmem((chunks, SIDE) + block, bf16),
            vmem((chunks, SIDE) + block, bf16),
            vmem((chunks, SIDE) + block, f32),
            vmem((chunks,) + block, bf16),
            vmem((chunks, 2, rows // 2, LANES), bf16),
            vmem((chunks,) + block, bf16),
            vmem((chunks,) + block, bf16),
            vmem((chunks,) + block, bf16),
            vmem((chunks,) + block, bf16),
            vmem((chunks,) + block, f32),
            vmem((chunks,) + block, bf16),
            vmem((chunks,) + block, bf16),
            vmem((8, LANES), f32),
            vmem((2, members, 1, LANES), f32),
            dma((members + chunks + 1,)),
            dma((chunks, 16)),
            dma((chunks, 16)),
            dma((chunks, 16)),
            dma((chunks, 16)),
            dma((chunks + 1,)),
            dma((chunks + 1,)),
            dma((2, members)),
            dma((2, members)),
        ],
        compiler_params=pltpu.CompilerParams(
            collective_id=0, has_side_effects=True, vmem_limit_bytes=60 * 2**20
        ),
    )(activations[0], targets[0], weights[0], lengths[0])
    return averaged[None]


def solution(mesh):
    return jax.shard_map(
        local,
        mesh=mesh,
        in_specs=(
            P("replica", "fsdp", None),
            P("replica", "fsdp", None),
            P("replica", "fsdp", None),
            P("replica", None),
        ),
        out_specs=P("replica", "fsdp", None),
        check_vma=False,
    )
```

```python
import functools

import jax
import jax.numpy as jnp
from jax import lax
from jax.experimental import pallas as pl
from jax.experimental.pallas import tpu as pltpu
from jax.sharding import PartitionSpec as P

SLOT = 64
STEP = 3
LANES = 128
SIDE = 4

learning_rate = 0.1
epsilon = 1e-06

MESH = pl.DeviceIdType.MESH
FIRST = ("z", "z", "x", "z")
(
    FROM_MINUS,
    FROM_PLUS,
    FIRST_MINUS,
    FIRST_PLUS,
    FIRST_FAR,
    PROJECT_HERE,
    PROJECT_MINUS,
    PROJECT_PLUS,
    PROJECT_FAR,
    GRAD_FAR,
    GRAD_SENT,
    GRAD_RELAYED,
    GRAD_HERE,
    RELAY,
    SECOND,
    FAR_MINUS,
    FAR_PLUS,
    FINISH,
    START,
    TRANSPOSE,
) = range(20)
ORDER = (
    (START, 0, 0), (START, 1, 0), (START, 3, 0), (TRANSPOSE, -1, 2),
    (FIRST_PLUS, 0, 0), (FIRST_MINUS, 0, 0), (START, 2, 0), (FIRST_MINUS, 1, 0),
    (TRANSPOSE, -1, 0), (FIRST_PLUS, 1, 0), (FIRST_FAR, 0, 0), (PROJECT_HERE, 0, 0),
    (FIRST_PLUS, 2, 0), (FROM_PLUS, 1, 1), (FIRST_MINUS, 2, 0), (FROM_MINUS, 0, 0),
    (FROM_PLUS, 0, 0), (FROM_PLUS, 0, 3), (TRANSPOSE, -1, 3), (FIRST_MINUS, 3, 0),
    (FROM_MINUS, 0, 1), (FIRST_FAR, 1, 0), (FROM_MINUS, 1, 3), (FROM_MINUS, 0, 3),
    (FROM_MINUS, 0, 2), (FIRST_FAR, 2, 0), (TRANSPOSE, -1, 1), (FROM_MINUS, 3, 0),
    (PROJECT_MINUS, 0, 0), (FROM_MINUS, 1, 0), (FROM_PLUS, 0, 2), (FIRST_PLUS, 3, 0),
    (FROM_PLUS, 0, 1), (PROJECT_HERE, 1, 0), (FROM_PLUS, 1, 0), (FROM_PLUS, 2, 1),
    (PROJECT_HERE, 2, 0), (PROJECT_PLUS, 0, 0), (FROM_PLUS, 1, 2), (FROM_PLUS, 3, 3),
    (FROM_MINUS, 3, 3), (FROM_PLUS, 3, 0), (FROM_PLUS, 2, 3), (FROM_MINUS, 2, 0),
    (FROM_MINUS, 1, 2), (FROM_PLUS, 1, 3), (FROM_MINUS, 1, 1), (FROM_MINUS, 2, 3),
    (FROM_MINUS, 2, 1), (PROJECT_MINUS, 1, 0), (FROM_PLUS, 2, 0), (FROM_PLUS, 2, 2),
    (PROJECT_FAR, 0, 0), (GRAD_FAR, 0, 0), (FIRST_FAR, 3, 0), (GRAD_SENT, 0, 0),
    (FROM_MINUS, 2, 2), (PROJECT_MINUS, 2, 0), (PROJECT_PLUS, 2, 0), (PROJECT_HERE, 3, 0),
    (PROJECT_PLUS, 1, 0), (PROJECT_FAR, 2, 0), (GRAD_FAR, 2, 0), (GRAD_RELAYED, 0, 0),
    (FROM_MINUS, 3, 1), (RELAY, 0, 2), (PROJECT_FAR, 1, 0), (GRAD_FAR, 1, 0),
    (GRAD_SENT, 2, 0), (FROM_MINUS, 3, 2), (FROM_PLUS, 3, 2), (GRAD_RELAYED, 2, 0),
    (PROJECT_MINUS, 3, 0), (RELAY, 0, 1), (GRAD_HERE, 0, 0), (GRAD_SENT, 1, 0),
    (GRAD_RELAYED, 1, 0), (RELAY, 2, 3), (RELAY, 1, 2), (FROM_PLUS, 3, 1),
    (RELAY, 0, 3), (PROJECT_PLUS, 3, 0), (SECOND, 0, 2), (RELAY, 1, 1),
    (RELAY, 2, 1), (PROJECT_FAR, 3, 0), (RELAY, 2, 2), (RELAY, 2, 0),
    (GRAD_FAR, 3, 0), (SECOND, 0, 1), (GRAD_HERE, 2, 0), (RELAY, 0, 0),
    (GRAD_SENT, 3, 0), (GRAD_RELAYED, 3, 0), (RELAY, 3, 2), (RELAY, 1, 3),
    (GRAD_HERE, 1, 0), (SECOND, 1, 2), (RELAY, 1, 0), (GRAD_HERE, 3, 0),
    (SECOND, 0, 3), (FAR_PLUS, 0, 0), (FAR_MINUS, 0, 0), (SECOND, 0, 0),
    (RELAY, 3, 1), (SECOND, 1, 1), (SECOND, 2, 2), (RELAY, 3, 3),
    (SECOND, 3, 2), (SECOND, 2, 0), (RELAY, 3, 0), (SECOND, 1, 3),
    (FAR_MINUS, 1, 0), (FAR_PLUS, 1, 0), (SECOND, 2, 3), (SECOND, 2, 1),
    (SECOND, 1, 0), (FINISH, 0, 0), (SECOND, 3, 3), (SECOND, 3, 1),
    (FAR_MINUS, 2, 0), (FAR_PLUS, 3, 0), (FAR_MINUS, 3, 0), (FAR_PLUS, 2, 0),
    (FINISH, 1, 0), (FINISH, 2, 0), (SECOND, 3, 0), (FINISH, 3, 0),
)


def kernel(
    bit,
    act,
    tgt,
    wgt,
    lens,
    out,
    a_v,
    at_v,
    t_v,
    wm,
    wp,
    w_all,
    keys,
    res,
    relay_out,
    relay_in,
    relay_own,
    fin_out_p,
    fin_out_m,
    fin_in_p,
    fin_in_m,
    own1,
    s2_out,
    s2_rin,
    f2_out_p,
    f2_out_m,
    f2_in_p,
    f2_in_m,
    g,
    g_low,
    gp,
    ss,
    ss_all,
    load_sem,
    ag_s,
    ag_r,
    rs_s,
    rs_r,
    y_s,
    y_r,
    ps_s,
    ps_r,
):
    members, tokens, rows = a_v.shape[0], act.shape[0], a_v.shape[2]
    depth = act.shape[1]
    chunks = w_all.shape[0]
    half = rows // 2
    sequences = tokens // SLOT
    fs = lax.axis_index("fsdp")
    rep = lax.axis_index("replica")
    x = lax.div(fs, SIDE)
    z = lax.rem(fs, SIDE)
    mask = 2**bit
    partner = rep + mask - 2 * mask * lax.rem(lax.div(rep, mask), 2)

    def step(v, k):
        return lax.rem(v + k, SIDE)

    def member(c, df, ds):
        if FIRST[c] == "z":
            return step(x, ds) * SIDE + step(z, df)
        return step(x, df) * SIDE + step(z, ds)

    def cut(c):
        return pl.ds(c * LANES, LANES)

    load_w = []
    for c in sorted(range(chunks), key=[o[1] for o in ORDER if o[0] == START].index):
        load_w.append(
            pltpu.make_async_copy(wgt.at[:, cut(c)], wm.at[:, cut(c)], load_sem.at[members + 1 + c])
        )
        load_w[-1].start()
    barrier = pltpu.get_barrier_semaphore()
    peer_y = {"replica": partner}
    for peer in (
        {"fsdp": step(x, 1) * SIDE + z},
        {"fsdp": step(x, 3) * SIDE + z},
        {"fsdp": x * SIDE + step(z, 1)},
        {"fsdp": x * SIDE + step(z, 3)},
        peer_y,
    ):
        pl.semaphore_signal(barrier, inc=1, device_id=peer, device_id_type=MESH)
    load_a = []
    for m in range(members):
        load_a.append(
            pltpu.make_async_copy(
                act.at[:, pl.ds(m * rows, rows)],
                a_v.at[m, pl.ds(0, tokens), :],
                load_sem.at[m],
            )
        )
        load_a[-1].start()
    load_t = pltpu.make_async_copy(tgt, t_v, load_sem.at[members])
    load_t.start()
    for c in range(chunks):
        load_w[c].wait()
    for c in range(chunks):
        w_all[c, fs] = wm[:, cut(c)].astype(jnp.bfloat16)
    pl.semaphore_wait(barrier, 5)

    sent = []

    def send(src, dst, send_sem, recv_sem, to):
        copy = pltpu.make_async_remote_copy(
            src_ref=src,
            dst_ref=dst,
            send_sem=send_sem,
            recv_sem=recv_sem,
            device_id=to,
            device_id_type=MESH,
        )
        copy.start()
        sent.append(copy)

    def arrived(dst, send_sem, recv_sem, to):
        pltpu.make_async_remote_copy(
            src_ref=dst,
            dst_ref=dst,
            send_sem=send_sem,
            recv_sem=recv_sem,
            device_id=to,
            device_id_type=MESH,
        ).wait_recv()

    def to_f(c, k):
        return {"fsdp": member(c, k, 0)}

    def to_s(c, k):
        return {"fsdp": member(c, 0, k)}

    def spread(c, j):
        block = w_all.at[c, member(c, j, 0)]
        send(block, block, ag_s.at[c, 4 + j], ag_r.at[c, 4 + j], to_s(c, 1))
        send(block, block, ag_s.at[c, 8 + j], ag_r.at[c, 8 + j], to_s(c, 3))

    def start(c, _):
        block = w_all.at[c, fs]
        send(block, block, ag_s.at[c, 0], ag_r.at[c, 0], to_f(c, 1))
        send(block, block, ag_s.at[c, 1], ag_r.at[c, 1], to_f(c, 3))
        spread(c, 0)

    def first_minus(c, _):
        block = w_all.at[c, member(c, 3, 0)]
        arrived(block, ag_s.at[c, 0], ag_r.at[c, 0], to_f(c, 1))
        part = block.at[pl.ds(0, half), :]
        send(part, part, ag_s.at[c, 2], ag_r.at[c, 2], to_f(c, 1))
        spread(c, 3)

    def first_plus(c, _):
        block = w_all.at[c, member(c, 1, 0)]
        arrived(block, ag_s.at[c, 1], ag_r.at[c, 1], to_f(c, 3))
        part = block.at[pl.ds(half, half), :]
        send(part, part, ag_s.at[c, 3], ag_r.at[c, 3], to_f(c, 3))
        spread(c, 1)

    def first_far(c, _):
        block = w_all.at[c, member(c, 2, 0)]
        arrived(block.at[pl.ds(0, half), :], ag_s.at[c, 2], ag_r.at[c, 2], to_f(c, 1))
        arrived(block.at[pl.ds(half, half), :], ag_s.at[c, 3], ag_r.at[c, 3], to_f(c, 3))
        spread(c, 2)

    def from_minus(c, j):
        block = w_all.at[c, member(c, j, 3)]
        arrived(block, ag_s.at[c, 4 + j], ag_r.at[c, 4 + j], to_s(c, 1))
        if j < 2:
            send(block, block, ag_s.at[c, 12 + j], ag_r.at[c, 12 + j], to_s(c, 1))

    def from_plus(c, j):
        block = w_all.at[c, member(c, j, 1)]
        arrived(block, ag_s.at[c, 8 + j], ag_r.at[c, 8 + j], to_s(c, 3))
        if j >= 2:
            send(block, block, ag_s.at[c, 12 + j], ag_r.at[c, 12 + j], to_s(c, 3))

    def project(c, ds, fresh=False):
        def body(j, carry):
            m = member(c, j, ds)
            keys[c] += jnp.dot(
                a_v[m, pl.ds(0, tokens), :], w_all[c, m], preferred_element_type=jnp.float32
            )
            return carry

        if fresh:
            keys[c] = jnp.zeros((tokens, LANES), jnp.float32)
        lax.fori_loop(0, SIDE, body, 0)

    def project_here(c, _):
        if not loaded:
            load_all()
        project(c, 0, fresh=True)

    def project_minus(c, _):
        project(c, 3)

    def project_plus(c, _):
        project(c, 1)

    def project_far(c, _):
        for j in range(SIDE):
            block = w_all.at[c, member(c, j, 2)]
            arrived(block, ag_s.at[c, 12 + j], ag_r.at[c, 12 + j], to_s(c, 1 if j < 2 else 3))
        project(c, 2)

    loaded = []

    def load_all():
        for copy in load_a:
            copy.wait()
        load_t.wait()
        pad = a_v.shape[1] - tokens
        if pad:
            for c in range(chunks):
                res[c, pl.ds(tokens, pad), :] = jnp.zeros((pad, LANES), res.dtype)
            for m in range(members):
                a_v[m, pl.ds(tokens, pad), :] = jnp.zeros((pad, rows), a_v.dtype)
        loaded.append(True)

    def transpose(_, k):
        def body(m, carry):
            at_v[m] = a_v[m].T
            return carry

        if not loaded:
            load_all()
        lax.fori_loop(k * (members // 4), (k + 1) * (members // 4), body, 0)

    def times_residual(c, j, ds):
        return jnp.dot(at_v[member(c, j, ds)], res[c], preferred_element_type=jnp.float32)

    def grad_far(c, _):
        for k in range(sequences):
            span = pl.ds(k * SLOT, SLOT)
            live = lax.broadcasted_iota(jnp.int32, (SLOT, LANES), 0) < lens[fs * sequences + k]
            wanted = t_v[span, c * LANES : (c + 1) * LANES].astype(jnp.float32)
            keys_out = keys[c, span, :] * depth ** (-0.5)
            res[c, span, :] = jnp.where(live, keys_out - wanted, 0.0).astype(jnp.bfloat16)

        def far(j, carry):
            relay_out[c, j] = times_residual(c, j, 2).astype(jnp.bfloat16)
            return carry

        lax.fori_loop(0, SIDE, far, 0)
        for j in range(SIDE):
            send(
                relay_out.at[c, j],
                relay_in.at[c, j],
                rs_s.at[c, j],
                rs_r.at[c, j],
                to_s(c, 1 if j < 2 else 3),
            )

    def grad_sent(c, _):
        def plus(j, carry):
            fin_out_p[c, j] = times_residual(c, j, 1).astype(jnp.bfloat16)
            return carry

        def minus(j, carry):
            fin_out_m[c, j] = times_residual(c, j, 3).astype(jnp.bfloat16)
            return carry

        lax.fori_loop(2, SIDE, plus, 0)
        for j in (2, 3):
            send_plus(c, j)
        lax.fori_loop(0, 2, minus, 0)
        for j in (0, 1):
            send_minus(c, j)

    def grad_relayed(c, _):
        def plus(j, carry):
            relay_own[c, j] = times_residual(c, j, 1)
            return carry

        def minus(j, carry):
            relay_own[c, j] = times_residual(c, j, 3)
            return carry

        lax.fori_loop(0, 2, plus, 0)
        lax.fori_loop(2, SIDE, minus, 0)

    def grad_here(c, _):
        def body(j, carry):
            own1[c, j] = times_residual(c, j, 0)
            return carry

        lax.fori_loop(0, SIDE, body, 0)

    def send_plus(c, j):
        send(
            fin_out_p.at[c, j], fin_in_m.at[c, j], rs_s.at[c, 4 + j], rs_r.at[c, 4 + j], to_s(c, 1)
        )

    def send_minus(c, j):
        send(
            fin_out_m.at[c, j], fin_in_p.at[c, j], rs_s.at[c, 8 + j], rs_r.at[c, 8 + j], to_s(c, 3)
        )

    def relay(c, j):
        arrived(relay_in.at[c, j], rs_s.at[c, j], rs_r.at[c, j], to_s(c, 1 if j < 2 else 3))
        total = (relay_own[c, j] + relay_in[c, j].astype(jnp.float32)).astype(jnp.bfloat16)
        if j < 2:
            fin_out_p[c, j] = total
            send_plus(c, j)
        else:
            fin_out_m[c, j] = total
            send_minus(c, j)

    def second(c, j):
        arrived(fin_in_m.at[c, j], rs_s.at[c, 4 + j], rs_r.at[c, 4 + j], to_s(c, 1))
        arrived(fin_in_p.at[c, j], rs_s.at[c, 8 + j], rs_r.at[c, 8 + j], to_s(c, 3))
        total = (
            own1[c, j] + fin_in_m[c, j].astype(jnp.float32) + fin_in_p[c, j].astype(jnp.float32)
        )
        if j != 2:
            own1[c, j] = total
            return
        s2_out[c] = total.astype(jnp.bfloat16)
        for k, to in ((0, 1), (1, 3)):
            send(
                s2_out.at[c, pl.ds(k * half, half), :],
                s2_rin.at[c, k],
                rs_s.at[c, 12 + k],
                rs_r.at[c, 12 + k],
                to_f(c, to),
            )

    upper, lower = pl.ds(0, half), pl.ds(half, half)

    def far_minus(c, _):
        arrived(s2_rin.at[c, 0], rs_s.at[c, 12], rs_r.at[c, 12], to_f(c, 1))
        f2_out_p[c, upper, :] = (
            own1[c, 1, upper, :] + s2_rin[c, 0].astype(jnp.float32)
        ).astype(jnp.bfloat16)
        f2_out_p[c, lower, :] = own1[c, 1, lower, :].astype(jnp.bfloat16)
        send(f2_out_p.at[c], f2_in_m.at[c], rs_s.at[c, 14], rs_r.at[c, 14], to_f(c, 1))

    def far_plus(c, _):
        arrived(s2_rin.at[c, 1], rs_s.at[c, 13], rs_r.at[c, 13], to_f(c, 3))
        f2_out_m[c, lower, :] = (
            own1[c, 3, lower, :] + s2_rin[c, 1].astype(jnp.float32)
        ).astype(jnp.bfloat16)
        f2_out_m[c, upper, :] = own1[c, 3, upper, :].astype(jnp.bfloat16)
        send(f2_out_m.at[c], f2_in_p.at[c], rs_s.at[c, 15], rs_r.at[c, 15], to_f(c, 3))

    done = []

    def finish(c, _):
        arrived(f2_in_m.at[c], rs_s.at[c, 14], rs_r.at[c, 14], to_f(c, 1))
        arrived(f2_in_p.at[c], rs_s.at[c, 15], rs_r.at[c, 15], to_f(c, 3))
        total = own1[c, 0] + f2_in_m[c].astype(jnp.float32) + f2_in_p[c].astype(jnp.float32)
        g[c] = total
        g_low[c] = total.astype(jnp.bfloat16)
        squares = jnp.sum((total * total).reshape(rows // 8, 8, LANES), axis=0)
        done.append(c)
        if len(done) > 1:
            squares += ss[...]
        ss[...] = squares
        if len(done) == chunks:
            share_squares()
        send(g_low.at[c], gp.at[c], y_s.at[c], y_r.at[c], peer_y)

    def share_squares():
        arrived(wp, y_s.at[chunks], y_r.at[chunks], peer_y)
        arrived(gp.at[done[0]], y_s.at[done[0]], y_r.at[done[0]], peer_y)
        ss_all[0, fs] = jnp.sum(ss[...], axis=0, keepdims=True)
        own = ss_all.at[0, fs]
        for k in range(members):
            to = {"replica": partner, "fsdp": lax.rem(fs + k, members)}
            send(own, ss_all.at[1, fs], ps_s.at[1, k], ps_r.at[1, fs], to)
        for k in range(1, members):
            to = {"fsdp": lax.rem(fs + k, members)}
            send(own, ss_all.at[0, fs], ps_s.at[0, k], ps_r.at[0, fs], to)

    steps = {
        START: start,
        FIRST_MINUS: first_minus,
        FIRST_PLUS: first_plus,
        FIRST_FAR: first_far,
        FROM_MINUS: from_minus,
        FROM_PLUS: from_plus,
        PROJECT_HERE: project_here,
        PROJECT_MINUS: project_minus,
        PROJECT_PLUS: project_plus,
        PROJECT_FAR: project_far,
        TRANSPOSE: transpose,
        GRAD_FAR: grad_far,
        GRAD_SENT: grad_sent,
        GRAD_RELAYED: grad_relayed,
        GRAD_HERE: grad_here,
        RELAY: relay,
        SECOND: second,
        FAR_MINUS: far_minus,
        FAR_PLUS: far_plus,
        FINISH: finish,
    }
    starts = 0
    for name, c, which in ORDER:
        steps[name](c, which)
        starts += name == START
        if name == START and starts == chunks:
            send(wm, wp, y_s.at[chunks], y_r.at[chunks], peer_y)

    entries = depth * LANES * chunks

    def scale(group):
        total = jnp.sum(ss_all[group], axis=(0, 1, 2), keepdims=True)[0]
        return (0.5 * learning_rate) * lax.rsqrt(total / entries + epsilon)

    for c in range(chunks):
        wp[:, cut(c)] = 0.5 * (wm[:, cut(c)] + wp[:, cut(c)])
    for k in range(1, members):
        m = lax.rem(fs + k, members)
        arrived(ss_all.at[0, m], ps_s.at[0, k], ps_r.at[0, m], peer_y)
    own_scale = scale(0)
    for c in done[1:]:
        arrived(gp.at[c], y_s.at[c], y_r.at[c], peer_y)
    for k in range(members):
        m = lax.rem(fs + k, members)
        arrived(ss_all.at[1, m], ps_s.at[1, k], ps_r.at[1, m], peer_y)
    partner_scale = scale(1)
    for c in range(chunks):
        out[:, cut(c)] = wp[:, cut(c)] - own_scale * g[c] - partner_scale * gp[c].astype(jnp.float32)
    for copy in sent:
        copy.wait_send()


def local(activations, targets, weights, lengths):
    tokens, depth = activations.shape[1:]
    rows, columns = weights.shape[1:]
    members = lax.axis_size("fsdp")
    chunks = columns // LANES
    bit = STEP % (lax.axis_size("replica").bit_length() - 1)
    padded = -(-tokens // LANES) * LANES
    bf16, f32 = jnp.bfloat16, jnp.float32
    vmem = pltpu.VMEM
    dma = pltpu.SemaphoreType.DMA
    block = (rows, LANES)
    any_spec = pl.BlockSpec(memory_space=pl.ANY)
    averaged = pl.pallas_call(
        functools.partial(kernel, bit),
        out_shape=jax.ShapeDtypeStruct((rows, columns), f32),
        in_specs=[any_spec, any_spec, any_spec, pl.BlockSpec(memory_space=pltpu.SMEM)],
        out_specs=pl.BlockSpec(memory_space=pltpu.VMEM),
        scratch_shapes=[
            vmem((members, padded, rows), bf16),
            vmem((members, rows, padded), bf16),
            vmem((tokens, columns), bf16),
            vmem((rows, columns), f32),
            vmem((rows, columns), f32),
            vmem((chunks, members) + block, bf16),
            vmem((chunks, tokens, LANES), f32),
            vmem((chunks, padded, LANES), bf16),
            vmem((chunks, SIDE) + block, bf16),
            vmem((chunks, SIDE) + block, bf16),
            vmem((chunks, SIDE) + block, f32),
            vmem((chunks, SIDE) + block, bf16),
            vmem((chunks, SIDE) + block, bf16),
            vmem((chunks, SIDE) + block, bf16),
            vmem((chunks, SIDE) + block, bf16),
            vmem((chunks, SIDE) + block, f32),
            vmem((chunks,) + block, bf16),
            vmem((chunks, 2, rows // 2, LANES), bf16),
            vmem((chunks,) + block, bf16),
            vmem((chunks,) + block, bf16),
            vmem((chunks,) + block, bf16),
            vmem((chunks,) + block, bf16),
            vmem((chunks,) + block, f32),
            vmem((chunks,) + block, bf16),
            vmem((chunks,) + block, bf16),
            vmem((8, LANES), f32),
            vmem((2, members, 1, LANES), f32),
            dma((members + chunks + 1,)),
            dma((chunks, 16)),
            dma((chunks, 16)),
            dma((chunks, 16)),
            dma((chunks, 16)),
            dma((chunks + 1,)),
            dma((chunks + 1,)),
            dma((2, members)),
            dma((2, members)),
        ],
        compiler_params=pltpu.CompilerParams(
            collective_id=0, has_side_effects=True, vmem_limit_bytes=60 * 2**20
        ),
    )(activations[0], targets[0], weights[0], lengths[0])
    return averaged[None]


def solution(mesh):
    return jax.shard_map(
        local,
        mesh=mesh,
        in_specs=(
            P("replica", "fsdp", None),
            P("replica", "fsdp", None),
            P("replica", "fsdp", None),
            P("replica", None),
        ),
        out_specs=P("replica", "fsdp", None),
        check_vma=False,
    )
```
